32 devices in a mesh: prow: 8 (over z, core), pcol: 4 (over y, x).
Axes of the slice: x: 2, y: 2, z: 4, core: 2. Of those that a mesh axis runs over, the one named last changes fastest.
Arguments:
- diag_block: float32 [256, 256], P('prow', 'pcol'), as said below
- panel: float32 [16384, 256], P('prow', 'pcol'), may hold values from -1.5 to 1.5
- slab: float32 [16384, 1024], P('prow', 'pcol'), may hold values from -6 to 6
Outputs:
- diag_factor: float32 [256, 256], P('prow', 'pcol')
- panel_factor: float32 [16384, 256], P('prow', 'pcol')
- slab_updated: float32 [16384, 1024], P('prow', 'pcol')
The draws below stay inside these ranges and needn't reach their ends.
Inputs may be any that keep to these rules, and one draw needn't show every extreme that they name: diag_block is symmetric positive definite.
All inputs are finite; a program needn't handle non-finite values.
Results may differ from the reference program's by a relative error of at most 0.0003.
Values sent between devices are 32-bit elements; how exact they have to be, the bound alone decides.
A program may use at most 64 MiB of HBM per device.

```python
import jax
import jax.numpy as jnp
from jax import lax

B = 256
LB = 8
PANEL = 16384
SLAB = 1024
N_PROW = 8
N_PCOL = 4


def draw_diag_block(key, part):
    base = jax.random.normal(jax.random.fold_in(key, 11), (B, B), jnp.float32)
    matrix = 2.0 * jnp.eye(B, dtype=jnp.float32) + jnp.dot(base, base.T) / B
    return 0.5 * (matrix + matrix.T)


def block_scale(rng, dims, shards, least, largest):
    loudness = 1.0
    for position, blocks in shards:
        draws = jax.random.uniform(jax.random.fold_in(jax.random.fold_in(rng, 6), position), (blocks,), jnp.float32, least / len(shards), largest / len(shards))
        loudness = loudness * jnp.repeat(jnp.exp(draws), dims[position] // blocks).reshape((-1,) + (1,) * (len(dims) - 1 - position))
    return loudness


def scatter_about(key, shape, deviation, bound, pieces=(), held_as=jnp.bfloat16):
    loudness = block_scale(key, shape, pieces, -0.22, 0.18) if pieces else 1.0
    array = jax.random.normal(key, shape, jnp.float32) * deviation * loudness
    return jnp.minimum(jnp.maximum(array, -bound), bound).astype(held_as)


def setup_inputs(seed: int = 0) -> dict:
    splits = jax.random.split(jax.random.key(seed), 4)
    diag_block = draw_diag_block(jax.random.fold_in(splits[3], 71), 0)
    panel = scatter_about(splits[1], (PANEL, B), 0.25, 1.5, ((0, 8), (1, 4)), jnp.float32)
    slab = scatter_about(splits[2], (PANEL, SLAB), 1.0, 6.0, ((0, 8), (1, 4)), jnp.float32)
    return {"diag_block": diag_block, "panel": panel, "slab": slab}


def reference(diag_block, panel, slab):
    diag_factor = jnp.linalg.cholesky(diag_block)
    panel_factor = jax.scipy.linalg.solve_triangular(diag_factor, panel.T, lower=True).T
    blocks = panel_factor.reshape(N_PROW * LB, B, B)
    group = LB * N_PROW // N_PCOL
    targets = jnp.arange(N_PCOL, dtype=jnp.int32) * group
    array_blocks = targets % N_PROW * LB + targets // N_PROW
    column_blocks = blocks[array_blocks]
    index = jnp.arange(PANEL, dtype=jnp.int32)
    block_index = index // B
    row_global = (block_index % LB * N_PROW + block_index // LB) * B + index % B
    slab_blocks = jnp.transpose(slab.reshape(PANEL, N_PCOL, B), (1, 0, 2))
    inner = jnp.arange(B, dtype=jnp.int32)

    def update(items):
        column_rows, slab_here, target = items
        product = jnp.dot(panel_factor.astype(jnp.float32), column_rows.T.astype(jnp.float32), precision=lax.Precision.HIGHEST, preferred_element_type=jnp.float32)
        col_global = target * B + inner
        keep_mask = row_global[:, None] >= col_global[None, :]
        return jnp.where(keep_mask, slab_here - product, slab_here)
    updated = lax.map(update, (column_blocks, slab_blocks, targets))
    slab_updated = jnp.transpose(updated, (1, 0, 2)).reshape(PANEL, SLAB)
    return (diag_factor, panel_factor, slab_updated)
```

```python
import functools

import jax
import jax.numpy as jnp
from jax import lax
from jax.experimental import pallas as pl
from jax.experimental.pallas import tpu as pltpu
from jax.sharding import PartitionSpec as P

HI = lax.Precision.HIGHEST
F32 = jnp.float32
NB = 64
EARLY = 3
VMEM_LIMIT = 24 * 1024 * 1024
MESH = pl.DeviceIdType.MESH


def dot_hi(a, b):
    return jnp.dot(a, b, precision=HI, preferred_element_type=F32)


def small(groups, width, one):
    lanes = 2 * width
    sub = lax.broadcasted_iota(jnp.int32, (8, lanes), 0)
    eight = range(8)
    count = width // 8

    def spread(x):
        return jnp.broadcast_to(x, (8, lanes))

    def column(x, j):
        return spread(x[:, j : j + 1])

    for g0 in range(count):
        base, first = groups[g0], 8 * g0
        columns = [column(base, first + k) * one for k in eight]
        d = {(m, k): spread(columns[k][m : m + 1, :]) for k in eight for m in range(k, 8)}
        rows = [spread(base[k : k + 1, :]) for k in eight]
        after = groups[g0 + 1] if g0 + 1 < count else None
        ahead = [column(after, first + k) for k in eight] if after is not None else None
        scales = []
        for k in eight:
            scale = lax.rsqrt(d[k, k])
            scales.append(scale)
            for m in range(k + 1, 8):
                d[m, k] = d[m, k] * scale
            for m in range(k + 1, 8):
                for q in range(k + 1, m + 1):
                    d[m, q] = d[m, q] - d[m, k] * d[q, k]
            rows[k] = rows[k] * scale
            for m in range(k + 1, 8):
                rows[m] = rows[m] - d[m, k] * rows[k]
            if ahead is not None:
                ahead[k] = ahead[k] * scale
                for m in range(k + 1, 8):
                    ahead[m] = ahead[m] - d[m, k] * ahead[k]
                after = after - ahead[k] * rows[k]
        solved = rows[0]
        for k in range(1, 8):
            solved = jnp.where(sub == k, rows[k], solved)
        groups[g0] = solved
        if ahead is not None:
            groups[g0 + 1] = after
        if g0 + 2 < count:
            back = [None] * 8
            for k in reversed(eight):
                total = rows[k]
                for m in range(k + 1, 8):
                    total = total - d[m, k] * back[m]
                back[k] = total * scales[k]
            for g in range(g0 + 2, count):
                terms = [column(groups[g], first + k) * back[k] for k in eight]
                while len(terms) > 1:
                    terms = [x + y for x, y in zip(terms[::2], terms[1::2])]
                groups[g] = groups[g] - terms[0]
    return jnp.concatenate(groups, axis=0)


def factor_block(matrix, upper, inverse, size, b, one):
    start, end = b * NB, (b + 1) * NB
    eye = (
        lax.broadcasted_iota(jnp.int32, (NB, NB), 0)
        == lax.broadcasted_iota(jnp.int32, (NB, NB), 1)
    ).astype(F32)
    right = matrix[start:end, start:]
    if b:
        left = upper[:start, start:end].T
        right = right - dot_hi(left, upper[:start, start:])
    if b > 1:
        last = start - NB
        below = dot_hi(upper[:last, last:start].T, inverse[:last, :last])
        inverse[last:start, :last] = -dot_hi(inverse[last:start, last:start], below)
    if b and end == size:
        for i in range(b):
            for j in range(i + 1, b):
                inverse[i * NB : (i + 1) * NB, j * NB : (j + 1) * NB] = jnp.zeros((NB, NB), F32)
        below = dot_hi(left, inverse[:start, :start])
    both = jnp.concatenate([right[:, :NB], eye], axis=1)
    solved = small([both[8 * g : 8 * g + 8] for g in range(NB // 8)], NB, one)
    triangle = (
        lax.broadcasted_iota(jnp.int32, (NB, NB), 1)
        >= lax.broadcasted_iota(jnp.int32, (NB, NB), 0)
    )
    upper[start:end, start:end] = jnp.where(triangle, solved[:, :NB], 0.0)
    own = solved[:, NB:]
    inverse[start:end, start:end] = own
    if end < size:
        upper[start:end, end:] = dot_hi(own, right[:, NB:])
    elif b:
        inverse[start:end, :start] = -dot_hi(own, below)


def split(x):
    high = x.astype(jnp.bfloat16)
    return high, (x - high.astype(F32)).astype(jnp.bfloat16)


def dot_split(a, b):
    (ah, al), (bh, bl) = a, b
    dot = functools.partial(jnp.dot, preferred_element_type=F32)
    return dot(ah, bh) + (dot(ah, bl) + dot(al, bh))


def main_kernel(
    rows, cols, group, fold,
    diag, panel, slab,
    diag_out, panel_out, slab_out,
    diag_own, tiles, gathered, matrix, upper, inverse, lower, strip_all, solved,
    own_sem, tile_send, tile_recv, wide_send, wide_recv,
    panel_send, panel_recv, strip_send, strip_recv, swap_send, mate_send, mate_recv,
):
    row, col = lax.axis_index("prow"), lax.axis_index("pcol")
    high, low = diag.shape
    size = matrix.shape[0]
    width, local_rows = panel.shape
    blocks = local_rows // size
    relay = cols == 4 and blocks % 2 == 0

    def remote(src, dst, send, recv, to):
        return pltpu.make_async_remote_copy(
            src_ref=src, dst_ref=dst, send_sem=send, recv_sem=recv,
            device_id=to, device_id_type=MESH,
        )

    def down(d):
        return {"prow": lax.rem(row + d, rows)}

    def across(d):
        return {"pcol": lax.rem(col + d, cols)}

    barrier = pltpu.get_barrier_semaphore()
    for d in range(1, rows):
        pl.semaphore_signal(barrier, inc=1, device_id=down(d), device_id_type=MESH)
    for d in range(1, cols):
        pl.semaphore_signal(barrier, inc=1, device_id=across(d), device_id_type=MESH)
    load = pltpu.make_async_copy(diag, diag_own, own_sem.at[0])
    load.start()
    own_panel = pltpu.make_async_copy(panel, gathered.at[col], own_sem.at[1])
    own_panel.start()
    own_slab = pltpu.make_async_copy(slab, slab_out, own_sem.at[2])
    own_slab.start()
    load.wait()
    step = high // fold
    packed = [diag_own[p * step : (p + 1) * step, :] for p in range(fold)]
    packed = jnp.concatenate(packed, axis=1) if fold > 1 else packed[0]
    tiles[pl.ds(col, 1), pl.ds(row, 1)] = packed[None, None]
    pl.semaphore_wait(barrier, rows + cols - 2)

    def needed(c):
        return ((c * low) // NB + 1) * NB // high

    my_tile = tiles.at[col, row]
    tile_copies = [
        remote(my_tile, my_tile, tile_send.at[d], tile_recv.at[row], down(d)) for d in range(1, rows)
    ]

    @pl.when(row < needed(col))
    def _():
        for copy in tile_copies:
            copy.start()

    def unit(u):
        return pl.ds(pl.multiple_of(u * size, size), size)

    def panel_copy(slot, u, to):
        return remote(
            panel.at[:, unit(u)], gathered.at[col, :, unit(u)],
            panel_send.at[slot, u], panel_recv.at[slot, u], to,
        )

    def arrived(slot, u):
        panel_copy(slot, u, across(1)).wait_recv()

    wanted = [c * group // rows for c in range(cols)]
    my_wanted = col * group // rows
    if relay:
        side, other = col + 1 - 2 * lax.rem(col, 2), lax.rem(col + 2, 4)
        opposite = 3 - col
        to_side, to_other = {"pcol": side}, {"pcol": other}
        near, far = list(range(blocks // 2)), list(range(blocks // 2, blocks))

        def order(k, mine, rest, neighbour):
            first = [wanted[k ^ 3]] if wanted[k ^ 3] in mine else []
            return list(dict.fromkeys(first + [wanted[neighbour]] + mine + rest))

        side_order = [order(k, near, far, k ^ 1) for k in range(4)]
        other_order = [order(k, far, near, k ^ 2) for k in range(4)]
        side_relay = [[u for u in side_order[c ^ 1] if u in near] for c in range(4)]
        other_relay = [[u for u in other_order[c ^ 2] if u in far] for c in range(4)]
        steps = blocks // 2

        def own_units(low_step, high_step):
            for c in range(4):

                @pl.when(col == c)
                def _():
                    for j in range(low_step, high_step):
                        panel_copy(0, side_order[c][j], to_side).start()
                        panel_copy(1, other_order[c][j], to_other).start()

        def forward(source, u, to):
            view = gathered.at[source, :, unit(u)]
            return remote(view, view, panel_send.at[2, u], panel_recv.at[2, u], to)

        def relay_step(j, waited):
            for c in range(4):

                @pl.when(col == c)
                def _():
                    u, v = side_relay[c][j], other_relay[c][j]
                    if not (waited and u == wanted[c]):
                        arrived(0, u)
                    forward(side, u, to_other).start()
                    if not (waited and v == wanted[c]):
                        arrived(1, v)
                    forward(other, v, to_side).start()

        own_units(0, EARLY)
    else:
        for u in range(blocks):
            for d in range(1, cols):
                panel_copy(d, u, across(d)).start()

    my_root = lax.rem(col * group, rows)
    core = lax.rem(row, 2)
    mate = {"prow": row + 1 - 2 * core}
    is_root = row == my_root
    same_chip = row // 2 == my_root // 2

    def strip_copy(k, d, src):
        return remote(src, strip_all.at[k], strip_send.at[k, d], strip_recv.at[k], down(d))

    def strip_half(k):
        return (k * 2) // cols

    def strip_each(k, act):
        def body(d, carry):
            to = lax.rem(row + d, rows)

            @pl.when((to // 2 == row // 2) | (lax.rem(to, 2) == strip_half(k)))
            def _():
                act(d)

            return carry

        lax.fori_loop(1, rows, body, 0)

    def strip_give(k, src):
        strip_each(k, lambda d: strip_copy(k, d, src).start())

    def strip_view(k):
        return gathered.at[k, :, unit(my_wanted)]

    @pl.when(is_root)
    def _():
        strip_give(col, panel.at[:, unit(my_wanted)])

    for r in range(rows):

        @pl.when((row != r) & (r < needed(col)))
        def _():
            there = tiles.at[col, r]
            remote(there, there, tile_send.at[0], tile_recv.at[r], down(1)).wait_recv()

    def wide(c, d):
        half = needed(c) // 2
        view = tiles.at[c, pl.ds(core * half, half)]
        if d is None:
            return remote(view, view, mate_send.at[c], mate_recv.at[c], mate)
        return remote(view, view, wide_send.at[d], wide_recv.at[c], across(d))

    for c in range(cols):

        @pl.when(col == c)
        def _():
            for d in range(1, cols):
                wide(c, d).start()

    if relay:
        for c in range(4):

            @pl.when(col == c)
            def _():
                u, v = side_relay[c][0], other_relay[c][0]
                arrived(0, u)
                forward(side, u, to_other).start()
                arrived(1, v)
                forward(other, v, to_side).start()
                for j in range(EARLY, blocks):
                    panel_copy(0, side_order[c][j], to_side).start()
                    panel_copy(1, other_order[c][j], to_other).start()
                if wanted[c] != u:
                    arrived(0, wanted[c])
                if wanted[c] != v:
                    arrived(1, wanted[c])

        @pl.when(is_root)
        def _():
            strip_give(side, strip_view(side))
            strip_give(other, strip_view(other))
    for c in range(cols):

        @pl.when(col != c)
        def _():
            wide(c, 1).wait_recv()
            wide(c, None).start()

    for c in range(cols):

        @pl.when(col != c)
        def _():
            wide(c, None).wait_recv()

    if not relay:
        for d in range(1, cols):
            arrived(d, my_wanted)

        @pl.when(is_root)
        def _():
            for d in range(1, cols):
                source = lax.rem(col + cols - d, cols)
                strip_give(source, strip_view(source))

    for c in range(cols):
        for r in range(needed(c)):
            for p in range(fold):
                top = r * high + p * step
                matrix[top : top + step, c * low : (c + 1) * low] = tiles[c, r][
                    :, p * low : (p + 1) * low
                ]
    one = jnp.where(row < rows, 1.0, 0.0).astype(F32)

    def swap(k):
        view = strip_all.at[k]
        return remote(view, view, swap_send.at[k], strip_recv.at[k], mate)

    for b in range(size // NB):
        factor_block(matrix, upper, inverse, size, b, one)
        if relay:
            if b == 0:
                arrived(2, my_wanted)

                @pl.when(is_root)
                def _():
                    strip_give(opposite, strip_view(opposite))

            for j in range(1, steps):
                if min(j - 1, size // NB - 2) == b:
                    relay_step(j, True)
        if b >= size // NB - 2:

            @pl.when(jnp.logical_not(same_chip))
            def _():
                for k in range(cols):
                    late = k == cols - 1 - col
                    now = late if b == size // NB - 1 else jnp.logical_not(late)

                    @pl.when((core == strip_half(k)) & now)
                    def _():
                        swap(k).wait_recv()
                        swap(k).start()

    for i in range(size // NB - 1):
        inverse[i * NB : (i + 1) * NB, size - NB :] = jnp.zeros((NB, NB), F32)
    own_panel.wait()

    @pl.when(is_root)
    def _():
        own = pltpu.make_async_copy(gathered.at[:, :, unit(my_wanted)], strip_all, own_sem.at[3])
        own.start()
        own.wait()

    for k in range(cols):

        @pl.when(jnp.logical_not(is_root) & (same_chip | (core != strip_half(k))))
        def _():
            swap(k).wait_recv()

    strip = split(dot_hi(inverse[...], strip_all[...].reshape(size, size)))
    inverse_parts = split(inverse[...])
    own_slab.wait()

    def update(i):
        here = slice(i * size, (i + 1) * size)
        full = gathered[:, :, here].reshape(size, size)
        factor = dot_split(inverse_parts, split(full))
        solved[...] = factor
        panel_out[:, here] = solved[pl.ds(pl.multiple_of(col * low, low), low), :]
        product = dot_split(split(factor.T), strip)
        shift = (i * rows + row - col * group) * size
        shape = (size, slab.shape[1])
        keep = (
            lax.broadcasted_iota(jnp.int32, shape, 0) + shift
            >= lax.broadcasted_iota(jnp.int32, shape, 1)
        )
        before = slab_out[here, :]
        slab_out[here, :] = jnp.where(keep, before - product, before)

    def settle(i):
        @pl.when(my_wanted != i)
        def _():
            if relay:
                arrived(1 if i in near else 0, i)
                arrived(2, i)
            else:
                for d in range(1, cols):
                    arrived(d, i)

    def finish_diag():
        for i in range(size // NB):
            for j in range(i, size // NB):
                at_i, at_j = slice(i * NB, (i + 1) * NB), slice(j * NB, (j + 1) * NB)
                lower[at_j, at_i] = upper[at_i, at_j].T
                if j > i:
                    lower[at_i, at_j] = jnp.zeros((NB, NB), F32)
        for c in range(cols):

            @pl.when(col == c)
            def _():
                start = pl.multiple_of(row * high, high)
                diag_out[...] = lower[pl.ds(start, high), c * low : (c + 1) * low]

    def drain():
        @pl.when(row < needed(col))
        def _():
            for copy in tile_copies:
                copy.wait_send()

        for c in range(cols):

            @pl.when(col == c)
            def _():
                for d in range(1, cols):
                    wide(c, d).wait_send()

            @pl.when(col != c)
            def _():
                wide(c, None).wait_send()

        for slot in range(3) if relay else range(1, cols):
            for u in range(blocks):
                panel_copy(slot, u, across(1)).wait_send()

        @pl.when(is_root)
        def _():
            for k in range(cols):
                strip_each(k, lambda d: strip_copy(k, d, strip_all.at[k]).wait_send())

        @pl.when(jnp.logical_not(same_chip))
        def _():
            for k in range(cols):

                @pl.when(core == strip_half(k))
                def _():
                    swap(k).wait_send()

    if relay:
        for i, j in zip(near, far):
            if i == blocks // 2 - 1:
                finish_diag()
                drain()
            settle(i)
            settle(j)
            update(i)
            update(j)
    else:
        for i in range(blocks):
            settle(i)
            update(i)
        finish_diag()
        drain()


def store_kernel(diag, panel, slab, diag_out, panel_out, slab_out, sems):
    copies = [
        pltpu.make_async_copy(slab, slab_out, sems.at[0]),
        pltpu.make_async_copy(panel, panel_out, sems.at[1]),
        pltpu.make_async_copy(diag, diag_out, sems.at[2]),
    ]
    for copy in copies:
        copy.start()
    for copy in copies:
        copy.wait()


def local(rows, cols, diag_block, panel, slab):
    high, low = diag_block.shape
    size = high * rows
    local_rows, width = panel.shape
    blocks = local_rows // size
    group = blocks * rows // cols
    fold = 128 // low if low < 128 and high * low % 1024 == 0 else 1
    hbm = pl.BlockSpec(memory_space=pltpu.HBM)
    vmem = pl.BlockSpec(memory_space=pltpu.VMEM)
    dma = pltpu.SemaphoreType.DMA
    shapes = [
        jax.ShapeDtypeStruct(diag_block.shape, F32),
        jax.ShapeDtypeStruct((width, local_rows), F32),
        jax.ShapeDtypeStruct(slab.shape, F32),
    ]
    slots = max(cols, 3)
    results = pl.pallas_call(
        functools.partial(main_kernel, rows, cols, group, fold),
        out_shape=shapes,
        in_specs=[hbm, hbm, hbm],
        out_specs=[vmem, vmem, vmem],
        scratch_shapes=[
            pltpu.VMEM((high, low), F32),
            pltpu.VMEM((cols, rows, high // fold, low * fold), F32),
            pltpu.VMEM((cols, width, local_rows), F32),
            pltpu.VMEM((size, size), F32),
            pltpu.VMEM((size, size), F32),
            pltpu.VMEM((size, size), F32),
            pltpu.VMEM((size, size), F32),
            pltpu.VMEM((cols, width, size), F32),
            pltpu.VMEM((size, size), F32),
            dma((4,)), dma((rows,)), dma((rows,)), dma((cols,)), dma((cols,)),
            dma((slots, blocks)), dma((slots, blocks)),
            dma((cols, rows)), dma((cols,)), dma((cols,)), dma((cols,)), dma((cols,)),
        ],
        compiler_params=pltpu.CompilerParams(
            collective_id=0, has_side_effects=True, vmem_limit_bytes=VMEM_LIMIT
        ),
        name="gather_update",
    )(*[pltpu.with_memory_space_constraint(x, pltpu.HBM) for x in (diag_block, panel.T, slab)])
    diag_out, panel_out, slab_out = pl.pallas_call(
        store_kernel,
        out_shape=shapes,
        in_specs=[vmem, vmem, vmem],
        out_specs=[hbm, hbm, hbm],
        scratch_shapes=[dma((3,))],
        compiler_params=pltpu.CompilerParams(vmem_limit_bytes=VMEM_LIMIT),
        name="store",
    )(*results)
    return diag_out, panel_out.T, slab_out


def solution(mesh):
    spec = P("prow", "pcol")
    return jax.shard_map(
        functools.partial(local, mesh.shape["prow"], mesh.shape["pcol"]),
        mesh=mesh,
        in_specs=(spec, spec, spec),
        out_specs=(spec, spec, spec),
        check_vma=False,
    )
```

```python
import functools

import jax
import jax.numpy as jnp
from jax import lax
from jax.experimental import pallas as pl
from jax.experimental.pallas import tpu as pltpu
from jax.sharding import PartitionSpec as P

HI = lax.Precision.HIGHEST
F32 = jnp.float32
NB = 64
EARLY = 3
VMEM_LIMIT = 24 * 1024 * 1024
MESH = pl.DeviceIdType.MESH


def dot_hi(a, b):
    return jnp.dot(a, b, precision=HI, preferred_element_type=F32)


def small(groups, width, one, midway):
    lanes = 2 * width
    sub = lax.broadcasted_iota(jnp.int32, (8, lanes), 0)
    eight = range(8)
    count = width // 8

    def spread(x):
        return jnp.broadcast_to(x, (8, lanes))

    def column(x, j):
        return spread(x[:, j : j + 1])

    for g0 in range(count):
        if g0 == count // 2:
            midway()
        base, first = groups[g0], 8 * g0
        columns = [column(base, first + k) * one for k in eight]
        d = {(m, k): spread(columns[k][m : m + 1, :]) for k in eight for m in range(k, 8)}
        rows = [spread(base[k : k + 1, :]) for k in eight]
        after = groups[g0 + 1] if g0 + 1 < count else None
        ahead = [column(after, first + k) for k in eight] if after is not None else None
        scales = []
        for k in eight:
            scale = lax.rsqrt(d[k, k])
            scales.append(scale)
            for m in range(k + 1, 8):
                d[m, k] = d[m, k] * scale
            for m in range(k + 1, 8):
                for q in range(k + 1, m + 1):
                    d[m, q] = d[m, q] - d[m, k] * d[q, k]
            rows[k] = rows[k] * scale
            for m in range(k + 1, 8):
                rows[m] = rows[m] - d[m, k] * rows[k]
            if ahead is not None:
                ahead[k] = ahead[k] * scale
                for m in range(k + 1, 8):
                    ahead[m] = ahead[m] - d[m, k] * ahead[k]
                after = after - ahead[k] * rows[k]
        solved = rows[0]
        for k in range(1, 8):
            solved = jnp.where(sub == k, rows[k], solved)
        groups[g0] = solved
        if ahead is not None:
            groups[g0 + 1] = after
        if g0 + 2 < count:
            back = [None] * 8
            for k in reversed(eight):
                total = rows[k]
                for m in range(k + 1, 8):
                    total = total - d[m, k] * back[m]
                back[k] = total * scales[k]
            for g in range(g0 + 2, count):
                terms = [column(groups[g], first + k) * back[k] for k in eight]
                while len(terms) > 1:
                    terms = [x + y for x, y in zip(terms[::2], terms[1::2])]
                groups[g] = groups[g] - terms[0]
    return jnp.concatenate(groups, axis=0)


def factor_block(matrix, upper, inverse, below, size, b, one, midway):
    start, end = b * NB, (b + 1) * NB
    eye = (
        lax.broadcasted_iota(jnp.int32, (NB, NB), 0)
        == lax.broadcasted_iota(jnp.int32, (NB, NB), 1)
    ).astype(F32)
    right = matrix[start:end, start:]
    if b:
        left = upper[:start, start:end].T
        right = right - dot_hi(left, upper[:start, start:])
    if b > 1:
        last = start - NB
        sums = dot_hi(upper[:last, last:start].T, inverse[:last, :last])
        inverse[last:start, :last] = -dot_hi(inverse[last:start, last:start], sums)
    if b and end == size:
        for i in range(b):
            for j in range(i + 1, b):
                inverse[i * NB : (i + 1) * NB, j * NB : (j + 1) * NB] = jnp.zeros((NB, NB), F32)
        below[:, :start] = dot_hi(left, inverse[:start, :start])
    both = jnp.concatenate([right[:, :NB], eye], axis=1)
    solved = small([both[8 * g : 8 * g + 8] for g in range(NB // 8)], NB, one, midway)
    triangle = (
        lax.broadcasted_iota(jnp.int32, (NB, NB), 1)
        >= lax.broadcasted_iota(jnp.int32, (NB, NB), 0)
    )
    upper[start:end, start:end] = jnp.where(triangle, solved[:, :NB], 0.0)
    own = solved[:, NB:]
    inverse[start:end, start:end] = own
    if end < size:
        upper[start:end, end:] = dot_hi(own, right[:, NB:])
    elif b:
        inverse[start:end, :start] = -dot_hi(own, below[:, :start])


def split(x):
    high = x.astype(jnp.bfloat16)
    return high, (x - high.astype(F32)).astype(jnp.bfloat16)


def dot_split(a, b):
    (ah, al), (bh, bl) = a, b
    dot = functools.partial(jnp.dot, preferred_element_type=F32)
    return dot(ah, bh) + (dot(ah, bl) + dot(al, bh))


def main_kernel(
    rows, cols, group, fold,
    diag, panel, slab,
    diag_out, panel_out, slab_out,
    diag_own, tiles, gathered, matrix, upper, inverse, lower, strip_all, below,
    own_sem, tile_send, tile_recv, wide_send, wide_recv,
    panel_send, panel_recv, strip_send, strip_recv, swap_send, mate_send, mate_recv,
):
    row, col = lax.axis_index("prow"), lax.axis_index("pcol")
    high, low = diag.shape
    size = matrix.shape[0]
    width, local_rows = panel.shape
    blocks = local_rows // size
    relay = cols == 4 and blocks % 2 == 0

    def remote(src, dst, send, recv, to):
        return pltpu.make_async_remote_copy(
            src_ref=src, dst_ref=dst, send_sem=send, recv_sem=recv,
            device_id=to, device_id_type=MESH,
        )

    def down(d):
        return {"prow": lax.rem(row + d, rows)}

    def across(d):
        return {"pcol": lax.rem(col + d, cols)}

    barrier = pltpu.get_barrier_semaphore()
    for d in range(1, rows):
        pl.semaphore_signal(barrier, inc=1, device_id=down(d), device_id_type=MESH)
    for d in range(1, cols):
        pl.semaphore_signal(barrier, inc=1, device_id=across(d), device_id_type=MESH)
    load = pltpu.make_async_copy(diag, diag_own, own_sem.at[0])
    load.start()
    own_panel = pltpu.make_async_copy(panel, gathered.at[col], own_sem.at[1])
    own_panel.start()
    own_slab = pltpu.make_async_copy(slab, slab_out, own_sem.at[2])
    own_slab.start()
    load.wait()
    step = high // fold
    packed = [diag_own[p * step : (p + 1) * step, :] for p in range(fold)]
    packed = jnp.concatenate(packed, axis=1) if fold > 1 else packed[0]
    tiles[pl.ds(col, 1), pl.ds(row, 1)] = packed[None, None]
    pl.semaphore_wait(barrier, rows + cols - 2)

    def needed(c):
        return ((c * low) // NB + 1) * NB // high

    my_tile = tiles.at[col, row]
    tile_copies = [
        remote(my_tile, my_tile, tile_send.at[d], tile_recv.at[row], down(d)) for d in range(1, rows)
    ]

    @pl.when(row < needed(col))
    def _():
        for copy in tile_copies:
            copy.start()

    def unit(u):
        return pl.ds(pl.multiple_of(u * size, size), size)

    def panel_copy(slot, u, to):
        return remote(
            panel.at[:, unit(u)], gathered.at[col, :, unit(u)],
            panel_send.at[slot, u], panel_recv.at[slot, u], to,
        )

    def arrived(slot, u):
        panel_copy(slot, u, across(1)).wait_recv()

    wanted = [c * group // rows for c in range(cols)]
    my_wanted = col * group // rows
    if relay:
        side, other = col + 1 - 2 * lax.rem(col, 2), lax.rem(col + 2, 4)
        opposite = 3 - col
        to_side, to_other = {"pcol": side}, {"pcol": other}
        near, far = list(range(blocks // 2)), list(range(blocks // 2, blocks))

        def order(k, mine, rest, neighbour):
            first = [wanted[k ^ 3]] if wanted[k ^ 3] in mine else []
            return list(dict.fromkeys(first + [wanted[neighbour]] + mine + rest))

        side_order = [order(k, near, far, k ^ 1) for k in range(4)]
        other_order = [order(k, far, near, k ^ 2) for k in range(4)]
        side_relay = [[u for u in side_order[c ^ 1] if u in near] for c in range(4)]
        other_relay = [[u for u in other_order[c ^ 2] if u in far] for c in range(4)]
        steps = blocks // 2

        def own_units(low_step, high_step):
            for c in range(4):

                @pl.when(col == c)
                def _():
                    for j in range(low_step, high_step):
                        panel_copy(0, side_order[c][j], to_side).start()
                        panel_copy(1, other_order[c][j], to_other).start()

        def forward(source, u, to):
            view = gathered.at[source, :, unit(u)]
            return remote(view, view, panel_send.at[2, u], panel_recv.at[2, u], to)

        def relay_step(j, waited):
            for c in range(4):

                @pl.when(col == c)
                def _():
                    u, v = side_relay[c][j], other_relay[c][j]
                    if not (waited and u == wanted[c]):
                        arrived(0, u)
                    forward(side, u, to_other).start()
                    if not (waited and v == wanted[c]):
                        arrived(1, v)
                    forward(other, v, to_side).start()

        own_units(0, EARLY)
    else:
        for u in range(blocks):
            for d in range(1, cols):
                panel_copy(d, u, across(d)).start()

    my_root = lax.rem(col * group, rows)
    core = lax.rem(row, 2)
    mate = {"prow": row + 1 - 2 * core}
    is_root = row == my_root
    same_chip = row // 2 == my_root // 2

    def strip_copy(k, d, src):
        return remote(src, strip_all.at[k], strip_send.at[k, d], strip_recv.at[k], down(d))

    def strip_half(k):
        return (k * 2) // cols

    def strip_each(k, act):
        def body(d, carry):
            to = lax.rem(row + d, rows)

            @pl.when((to // 2 == row // 2) | (lax.rem(to, 2) == strip_half(k)))
            def _():
                act(d)

            return carry

        lax.fori_loop(1, rows, body, 0)

    def strip_give(k, src):
        strip_each(k, lambda d: strip_copy(k, d, src).start())

    def strip_view(k):
        return gathered.at[k, :, unit(my_wanted)]

    @pl.when(is_root)
    def _():
        strip_give(col, panel.at[:, unit(my_wanted)])

    for r in range(rows):

        @pl.when((row != r) & (r < needed(col)))
        def _():
            there = tiles.at[col, r]
            remote(there, there, tile_send.at[0], tile_recv.at[r], down(1)).wait_recv()

    def wide(c, d):
        half = needed(c) // 2
        view = tiles.at[c, pl.ds(core * half, half)]
        if d is None:
            return remote(view, view, mate_send.at[c], mate_recv.at[c], mate)
        return remote(view, view, wide_send.at[d], wide_recv.at[c], across(d))

    for c in range(cols):

        @pl.when(col == c)
        def _():
            for d in range(1, cols):
                wide(c, d).start()

    if relay:
        for c in range(4):

            @pl.when(col == c)
            def _():
                u, v = side_relay[c][0], other_relay[c][0]
                arrived(0, u)
                forward(side, u, to_other).start()
                arrived(1, v)
                forward(other, v, to_side).start()
                for j in range(EARLY, blocks):
                    panel_copy(0, side_order[c][j], to_side).start()
                    panel_copy(1, other_order[c][j], to_other).start()
                if wanted[c] != u:
                    arrived(0, wanted[c])
                if wanted[c] != v:
                    arrived(1, wanted[c])

        @pl.when(is_root)
        def _():
            strip_give(side, strip_view(side))
            strip_give(other, strip_view(other))
    for c in range(cols):

        @pl.when(col != c)
        def _():
            wide(c, 1).wait_recv()
            wide(c, None).start()

    for c in range(cols):

        @pl.when(col != c)
        def _():
            wide(c, None).wait_recv()

    if not relay:
        for d in range(1, cols):
            arrived(d, my_wanted)

        @pl.when(is_root)
        def _():
            for d in range(1, cols):
                source = lax.rem(col + cols - d, cols)
                strip_give(source, strip_view(source))

    for c in range(cols):
        for r in range(needed(c)):
            for p in range(fold):
                top = r * high + p * step
                matrix[top : top + step, c * low : (c + 1) * low] = tiles[c, r][
                    :, p * low : (p + 1) * low
                ]
    if relay and steps > 1:
        relay_step(1, True)
    one = jnp.where(row < rows, 1.0, 0.0).astype(F32)

    def swap(k):
        view = strip_all.at[k]
        return remote(view, view, swap_send.at[k], strip_recv.at[k], mate)

    last = size // NB - 1

    def swap_part(final):
        @pl.when(jnp.logical_not(same_chip))
        def _():
            for k in range(cols):
                late = k == cols - 1 - col

                @pl.when((core == strip_half(k)) & (late if final else jnp.logical_not(late)))
                def _():
                    swap(k).wait_recv()
                    swap(k).start()

    def midway(b):
        if b == last:
            swap_part(True)
        elif b == last - 1:
            swap_part(False)
        elif relay and b > 0:
            for j in range(3, steps):
                if min(j - 2, last - 2) == b:
                    relay_step(j, True)

    for b in range(last + 1):
        factor_block(
            matrix, upper, inverse, below, size, b, one, functools.partial(midway, b)
        )
        if relay and b == 0:
            arrived(2, my_wanted)

            @pl.when(is_root)
            def _():
                strip_give(opposite, strip_view(opposite))

            if steps > 2:
                relay_step(2, True)

    for i in range(size // NB - 1):
        inverse[i * NB : (i + 1) * NB, size - NB :] = jnp.zeros((NB, NB), F32)
    own_panel.wait()

    @pl.when(is_root)
    def _():
        own = pltpu.make_async_copy(gathered.at[:, :, unit(my_wanted)], strip_all, own_sem.at[3])
        own.start()
        own.wait()

    for k in range(cols):

        @pl.when(jnp.logical_not(is_root) & (same_chip | (core != strip_half(k))))
        def _():
            swap(k).wait_recv()

    whole = inverse[...]
    strip = split(dot_hi(whole.T, dot_hi(whole, strip_all[...].reshape(size, size))))
    own_rows = split(inverse[pl.ds(pl.multiple_of(col * low, low), low), :])
    own_slab.wait()

    def update(i):
        here = slice(i * size, (i + 1) * size)
        full = gathered[:, :, here].reshape(size, size)
        panel_out[:, here] = dot_split(own_rows, split(full))
        product = dot_split(split(full.T), strip)
        shift = (i * rows + row - col * group) * size
        shape = (size, slab.shape[1])
        keep = (
            lax.broadcasted_iota(jnp.int32, shape, 0) + shift
            >= lax.broadcasted_iota(jnp.int32, shape, 1)
        )
        before = slab_out[here, :]
        slab_out[here, :] = jnp.where(keep, before - product, before)

    def settle(i):
        @pl.when(my_wanted != i)
        def _():
            if relay:
                arrived(1 if i in near else 0, i)
                arrived(2, i)
            else:
                for d in range(1, cols):
                    arrived(d, i)

    def finish_diag():
        for i in range(size // NB):
            for j in range(i, size // NB):
                at_i, at_j = slice(i * NB, (i + 1) * NB), slice(j * NB, (j + 1) * NB)
                lower[at_j, at_i] = upper[at_i, at_j].T
                if j > i:
                    lower[at_i, at_j] = jnp.zeros((NB, NB), F32)
        for c in range(cols):

            @pl.when(col == c)
            def _():
                start = pl.multiple_of(row * high, high)
                diag_out[...] = lower[pl.ds(start, high), c * low : (c + 1) * low]

    def drain():
        @pl.when(row < needed(col))
        def _():
            for copy in tile_copies:
                copy.wait_send()

        for c in range(cols):

            @pl.when(col == c)
            def _():
                for d in range(1, cols):
                    wide(c, d).wait_send()

            @pl.when(col != c)
            def _():
                wide(c, None).wait_send()

        for slot in range(3) if relay else range(1, cols):
            for u in range(blocks):
                panel_copy(slot, u, across(1)).wait_send()

        @pl.when(is_root)
        def _():
            for k in range(cols):
                strip_each(k, lambda d: strip_copy(k, d, strip_all.at[k]).wait_send())

        @pl.when(jnp.logical_not(same_chip))
        def _():
            for k in range(cols):

                @pl.when(core == strip_half(k))
                def _():
                    swap(k).wait_send()

    if relay:
        for i, j in zip(near, far):
            if i == blocks // 2 - 1:
                finish_diag()
                drain()
            settle(i)
            settle(j)
            update(i)
            update(j)
    else:
        for i in range(blocks):
            settle(i)
            update(i)
        finish_diag()
        drain()


def store_kernel(diag, panel, slab, diag_out, panel_out, slab_out, sems):
    copies = [
        pltpu.make_async_copy(slab, slab_out, sems.at[0]),
        pltpu.make_async_copy(panel, panel_out, sems.at[1]),
        pltpu.make_async_copy(diag, diag_out, sems.at[2]),
    ]
    for copy in copies:
        copy.start()
    for copy in copies:
        copy.wait()


def local(rows, cols, diag_block, panel, slab):
    high, low = diag_block.shape
    size = high * rows
    local_rows, width = panel.shape
    blocks = local_rows // size
    group = blocks * rows // cols
    fold = 128 // low if low < 128 and high * low % 1024 == 0 else 1
    hbm = pl.BlockSpec(memory_space=pltpu.HBM)
    vmem = pl.BlockSpec(memory_space=pltpu.VMEM)
    dma = pltpu.SemaphoreType.DMA
    shapes = [
        jax.ShapeDtypeStruct(diag_block.shape, F32),
        jax.ShapeDtypeStruct((width, local_rows), F32),
        jax.ShapeDtypeStruct(slab.shape, F32),
    ]
    slots = max(cols, 3)
    results = pl.pallas_call(
        functools.partial(main_kernel, rows, cols, group, fold),
        out_shape=shapes,
        in_specs=[hbm, hbm, hbm],
        out_specs=[vmem, vmem, vmem],
        scratch_shapes=[
            pltpu.VMEM((high, low), F32),
            pltpu.VMEM((cols, rows, high // fold, low * fold), F32),
            pltpu.VMEM((cols, width, local_rows), F32),
            pltpu.VMEM((size, size), F32),
            pltpu.VMEM((size, size), F32),
            pltpu.VMEM((size, size), F32),
            pltpu.VMEM((size, size), F32),
            pltpu.VMEM((cols, width, size), F32),
            pltpu.VMEM((NB, size), F32),
            dma((4,)), dma((rows,)), dma((rows,)), dma((cols,)), dma((cols,)),
            dma((slots, blocks)), dma((slots, blocks)),
            dma((cols, rows)), dma((cols,)), dma((cols,)), dma((cols,)), dma((cols,)),
        ],
        compiler_params=pltpu.CompilerParams(
            collective_id=0, has_side_effects=True, vmem_limit_bytes=VMEM_LIMIT
        ),
        name="gather_update",
    )(*[pltpu.with_memory_space_constraint(x, pltpu.HBM) for x in (diag_block, panel.T, slab)])
    diag_out, panel_out, slab_out = pl.pallas_call(
        store_kernel,
        out_shape=shapes,
        in_specs=[vmem, vmem, vmem],
        out_specs=[hbm, hbm, hbm],
        scratch_shapes=[dma((3,))],
        compiler_params=pltpu.CompilerParams(vmem_limit_bytes=VMEM_LIMIT),
        name="store",
    )(*results)
    return diag_out, panel_out.T, slab_out


def solution(mesh):
    spec = P("prow", "pcol")
    return jax.shard_map(
        functools.partial(local, mesh.shape["prow"], mesh.shape["pcol"]),
        mesh=mesh,
        in_specs=(spec, spec, spec),
        out_specs=(spec, spec, spec),
        check_vma=False,
    )
```
